32 devices in a mesh: groups: 2 (over y), frames: 4 (over z), code: 2 (over x), head: 2 (over core).
Axes of the slice: x: 2, y: 2, z: 4, core: 2. Of those that a mesh axis runs over, the one named last changes fastest.
Arguments:
- video: bfloat16 [256, 16, 1024], P(('code', 'head'), ('groups', 'frames')), parts along dimension 1, may hold values from -6 to 6
- conv_weight: bfloat16 [3, 1024, 1024], replicated, may hold values from -0.109375 to 0.109375
- norm_gain: float32 [1024], replicated, may hold values from 0.1 to 1.9
- qkv_weight: bfloat16 [1024, 3, 1024], P(None, None, ('code', 'head')), may hold values from -1 to 1
- out_weight: bfloat16 [1024, 1024], P(('code', 'head')), may hold values from -0.1875 to 0.1875
- latent_weight: bfloat16 [1024, 16], replicated, may hold values from -0.1875 to 0.1875
- codebook: bfloat16 [16, 65536], P(None, ('code', 'head')), may hold values from -9 to 9
- reference_codes: int32 [256, 16], P(None, ('groups', 'frames')), parts along dimension 1, may hold values from 0 to 65535
Outputs:
- encoded: bfloat16 [256, 16, 1024], P(('code', 'head'), ('groups', 'frames')), parts along dimension 1
- nearest_distance: float32 [256, 16], P(('code', 'head'), ('groups', 'frames')), parts along dimension 1
- reference_gap: float32 [256, 16], P(('code', 'head'), ('groups', 'frames')), parts along dimension 1
The draws below stay inside these ranges and needn't reach their ends.
There are 2 independent parts, one for each index of `groups`. The reference program is written for one: setup_inputs(seed, part) draws one part's arguments, and reference() takes and returns one part's arrays. A program takes and returns all parts, laid end to end along the dimension named above; an argument that names none is the same for every part. Nothing has to cross between parts.
All inputs are finite; a program needn't handle non-finite values.
Results may differ from the reference program's by a relative error of at most 0.015.
Values may be sent and summed in bfloat16 or wider, within the bound.
No kernel may reach another device: no remote copies, remote signals or barrier semaphores. Data moves between devices by JAX's collectives and lax.ppermute only.
A program may use at most 64 MiB of HBM per device.

```python
import math
import jax
import jax.numpy as jnp
from jax import lax

D = 1024
HEADS = 16
CODES = 65536
CDIM = 16
S = 256
F = 8


def draw_qkv_weight(key, part):
    first = jax.random.fold_in(jax.random.fold_in(key, 11), 0)
    base = jax.random.normal(first, (D, 3, D), jnp.float32) / math.sqrt(D)
    base = jnp.clip(base, -1.0, 1.0)
    return base.astype(jnp.bfloat16)


def with_ends(array, key, smallest, largest):
    dims = array.shape
    spot = [jax.random.randint(jax.random.fold_in(key, axis), (), 0, dims[axis]) for axis in range(len(dims))]
    array = array.at[tuple(spot)].set(smallest)
    longest = dims.index(max(dims))
    spot[longest] = (spot[longest] + 1) % dims[longest]
    return array.at[tuple(spot)].set(largest)


def block_scale(rng, dims, pieces, low, high):
    factor_of = 1.0
    for dim, parts in pieces:
        draws = jax.random.uniform(jax.random.fold_in(jax.random.fold_in(rng, 6), dim), (parts,), jnp.float32, low / len(pieces), high / len(pieces))
        factor_of = factor_of * jnp.repeat(jnp.exp(draws), dims[dim] // parts).reshape((-1,) + (1,) * (len(dims) - 1 - dim))
    return factor_of


def scatter_about(rng, extent, spread, most, pieces=(), kind=jnp.bfloat16):
    result = jax.random.normal(rng, extent, jnp.float32) * spread
    if len(pieces) > 0:
        result = block_scale(rng, extent, pieces, -0.22, 0.18) * result
    return jnp.clip(result, min=-most, max=most).astype(kind)


def setup_inputs(seed: int = 0, part: int = 0) -> dict:
    key_list = jax.random.split(jax.random.key(seed), 9)
    part_splits = jax.random.split(jax.random.fold_in(key_list[8], part), 9)
    return {
        "video": scatter_about(part_splits[0], (S, F, D), 1.0, 6.0, ((0, 4), (1, 4))),
        "conv_weight": scatter_about(key_list[1], (3, D, D), (3 * D) ** -0.5, 0.109375),
        "norm_gain": jnp.clip(1.0 + 0.18 * jax.random.normal(key_list[2], (D,), jnp.float32), 0.1, 1.9),
        "qkv_weight": draw_qkv_weight(jax.random.fold_in(key_list[8], 71), part),
        "out_weight": scatter_about(key_list[4], (D, D), D ** -0.5, 0.1875, ((0, 4),)),
        "latent_weight": scatter_about(key_list[5], (D, CDIM), D ** -0.5, 0.1875),
        "codebook": scatter_about(key_list[6], (CDIM, CODES), 1.5, 9.0, ((1, 4),)),
        "reference_codes": with_ends(jax.random.randint(part_splits[7], (S, F), 0, CODES), jax.random.fold_in(part_splits[7], 1), 0, CODES - 1).astype(jnp.int32),
    }


EPSILON = 1e-06

def conv_block(video, conv_weight):
    positions, frame_count, model_width = video.shape
    zeros_front = jnp.zeros((positions, 2, model_width), video.dtype)
    padded = jnp.concatenate([zeros_front, video], axis=1)
    stacked = jnp.concatenate([padded[:, 2:], padded[:, 1:-1], padded[:, :-2]], axis=2)
    mixed = jnp.dot(stacked.reshape(-1, 3 * model_width), conv_weight.reshape(3 * model_width, model_width), preferred_element_type=jnp.float32)
    return (video.reshape(-1, model_width).astype(jnp.float32) + jax.nn.silu(mixed)).astype(jnp.bfloat16)

def normalize(block_input, norm_gain):
    values32 = block_input.astype(jnp.float32)
    mean_square = lax.optimization_barrier(jnp.mean(values32 * values32, axis=-1, keepdims=True))
    return (values32 * lax.rsqrt(mean_square + EPSILON) * norm_gain).astype(jnp.bfloat16)

def attend(queries, keys, values, frame_of):
    head_count, token_count, head_dim = queries.shape
    block = math.gcd(token_count, 1024)
    score_scale = 1.0 / math.sqrt(head_dim)

    def one_head(operands):
        head_q, head_k, head_v = operands

        def one_block(block_index):
            rows_q = lax.dynamic_slice_in_dim(head_q, block_index * block, block, 0)
            frames_q = lax.dynamic_slice_in_dim(frame_of, block_index * block, block, 0)
            scores = jnp.dot(rows_q, head_k.T, preferred_element_type=jnp.float32) * score_scale
            allowed = frame_of[None, :] <= frames_q[:, None]
            highest = lax.optimization_barrier(jnp.max(jnp.where(allowed, scores, -1e+30), axis=1, keepdims=True))
            weights = jnp.where(allowed, jnp.exp(scores - highest), 0.0)
            denominator = lax.optimization_barrier(jnp.sum(weights, axis=1, keepdims=True))
            return jnp.dot(weights.astype(jnp.bfloat16), head_v, preferred_element_type=jnp.float32) / denominator
        blocks = lax.map(one_block, jnp.arange(token_count // block, dtype=jnp.int32))
        return blocks.reshape(token_count, head_dim).astype(jnp.bfloat16)
    return lax.map(one_head, (queries, keys, values))

def search(latent, codebook, reference_codes):
    code_dim, code_count = codebook.shape
    block = math.gcd(code_count, 4096)
    latent32 = latent.astype(jnp.float32)
    squares = lax.optimization_barrier(jnp.sum(latent32 * latent32, axis=1))
    wanted = reference_codes.reshape(-1)

    def visit(running, block_index):
        least, chosen = running
        codes = lax.dynamic_slice_in_dim(codebook, block_index * block, block, 1)
        codes32 = codes.astype(jnp.float32)
        code_squares = lax.optimization_barrier(jnp.sum(codes32 * codes32, axis=0))
        dots = jnp.dot(latent, codes, preferred_element_type=jnp.float32)
        distance = (squares[:, None] - 2.0 * dots + code_squares[None, :]) / code_dim
        labels = block_index * block + jnp.arange(block, dtype=jnp.int32)
        least = jnp.minimum(least, lax.optimization_barrier(jnp.min(distance, axis=1)))
        chosen = chosen + lax.optimization_barrier(jnp.sum(jnp.where(labels[None, :] == wanted[:, None], distance, 0.0), axis=1))
        return ((least, chosen), None)
    start_state = (jnp.full(squares.shape, 1e+30, jnp.float32), jnp.zeros(squares.shape, jnp.float32))
    (least, chosen), unused = lax.scan(visit, start_state, jnp.arange(code_count // block, dtype=jnp.int32))
    return (least, chosen)

def reference(video, conv_weight, norm_gain, qkv_weight, out_weight, latent_weight, codebook, reference_codes):
    positions, frame_count, model_width = video.shape
    token_count = positions * frame_count
    head_dim = model_width // HEADS
    block_input = conv_block(video, conv_weight)
    normed = normalize(block_input, norm_gain)
    triple = jnp.dot(normed, qkv_weight.reshape(model_width, 3 * model_width), preferred_element_type=jnp.float32).astype(jnp.bfloat16)
    triple = triple.reshape(token_count, 3, HEADS, head_dim)
    queries = jnp.transpose(triple[:, 0], (1, 0, 2))
    keys = jnp.transpose(triple[:, 1], (1, 0, 2))
    values = jnp.transpose(triple[:, 2], (1, 0, 2))
    frame_of = jnp.arange(token_count, dtype=jnp.int32) % frame_count
    heads_out = attend(queries, keys, values, frame_of)
    attended = jnp.transpose(heads_out, (1, 0, 2)).reshape(token_count, model_width)
    projected = jnp.dot(attended, out_weight, preferred_element_type=jnp.float32)
    encoded = (block_input.astype(jnp.float32) + projected).astype(jnp.bfloat16)
    latent = jnp.dot(encoded, latent_weight, preferred_element_type=jnp.float32).astype(jnp.bfloat16)
    least, chosen = search(latent, codebook, reference_codes)
    return (encoded.reshape(positions, frame_count, model_width), least.reshape(positions, frame_count), (chosen - least).reshape(positions, frame_count))
```

```python
import functools
import math

import jax
import jax.numpy as jnp
from jax import lax
from jax.experimental import pallas as pl
from jax.experimental.pallas import tpu as pltpu
from jax.sharding import PartitionSpec as P

HEADS = 16
EPSILON = 1e-06
LANES = 128
EXT = 32

VMEM = pl.BlockSpec(memory_space=pltpu.VMEM)
SMEM = pl.BlockSpec(memory_space=pltpu.SMEM)


def call(kernel, out_shape, operands, scratch=(), scalars=0, flops=0, moved=0, name=None, limit=20):
    single = not isinstance(out_shape, (tuple, list))
    specs = [SMEM] * scalars + [VMEM] * (len(operands) - scalars)
    return pl.pallas_call(
        kernel,
        out_shape=out_shape,
        in_specs=specs,
        out_specs=VMEM if single else [VMEM] * len(out_shape),
        scratch_shapes=list(scratch),
        compiler_params=pltpu.CompilerParams(vmem_limit_bytes=limit << 20),
        cost_estimate=pl.CostEstimate(flops=flops, bytes_accessed=moved, transcendentals=0),
        name=name,
    )(*operands)


def shifted(block, axis, distance, around):
    size = lax.axis_size(axis)
    if around:
        route = [(i, (i + distance) % size) for i in range(size)]
    else:
        route = [(i, i + distance) for i in range(size) if i + distance < size]
    return lax.ppermute(block, axis, route)


def conv_kernel(count, keep, *refs):
    currents, earliers = refs[:count], refs[count : 2 * count]
    w_ref, gain_ref = refs[2 * count : 2 * count + 2]
    outs = refs[2 * count + 2 : -1]
    block_ref = refs[-1]
    rows, width = currents[0].shape
    half = rows // 2
    taps = [[], [], []]
    for cur, prev in zip(currents, earliers):
        taps[0] += [cur[...]]
        taps[1] += [prev[half:, :], cur[:half, :]]
        taps[2] += [prev[...]]
    taps = [t[0] if len(t) == 1 else jnp.concatenate(t, axis=0) for t in taps]
    chunk = min(width, 256)
    total = jnp.zeros((count * rows, 1), jnp.float32)
    for j in range(0, width, chunk):
        mixed = sum(
            jnp.dot(taps[k], w_ref[k, :, j : j + chunk], preferred_element_type=jnp.float32)
            for k in range(3)
        )
        silu = mixed / (1.0 + jnp.exp(-mixed))
        block = (taps[0][:, j : j + chunk].astype(jnp.float32) + silu).astype(jnp.bfloat16)
        block_ref[:, j : j + chunk] = block
        block32 = block.astype(jnp.float32)
        total = total + jnp.sum(block32 * block32, axis=1, keepdims=True)
    inverse = lax.rsqrt(total / width + EPSILON)
    for i in range(count):
        part = slice(i * rows, (i + 1) * rows)
        block32 = block_ref[part, :].astype(jnp.float32)
        outs[i][...] = (block32 * inverse[part] * gain_ref[...]).astype(jnp.bfloat16)
    if keep:
        outs[count][...] = block_ref[:rows, :]


def conv_norm(pairs, conv_weight, gain, keep, name):
    count = len(pairs)
    rows, width = pairs[0][0].shape
    shape = jax.ShapeDtypeStruct((rows, width), jnp.bfloat16)
    return call(
        functools.partial(conv_kernel, count, keep),
        [shape] * (count + keep),
        [p[0] for p in pairs] + [p[1] for p in pairs] + [conv_weight, gain],
        scratch=[pltpu.VMEM((count * rows, width), jnp.bfloat16)],
        flops=6 * count * rows * width * width,
        moved=conv_weight.size * 2,
        name=name,
        limit=16,
    )


def slab_kernel(ncol, first, last, head_dim, *refs):
    refs = list(refs)
    valid_ref = None if first else refs.pop(0)
    columns = [refs.pop(0) for _ in range(ncol)]
    w_ref = refs.pop(0)
    if first:
        q_old = acc_old = top_old = None
    else:
        q_old, acc_old, top_old = refs.pop(0), refs.pop(0), refs.pop(0)
    if last:
        outs = [refs.pop(0) for _ in range(ncol)]
        if first:
            q_new = None
        acc_new = top_new = None
    else:
        if first:
            q_new = refs.pop(0)
        acc_new, top_new = refs.pop(0), refs.pop(0)
    x_ref = refs.pop(0)
    if last:
        acc_new, top_new = refs.pop(0), refs.pop(0)
        if first:
            q_new = refs.pop(0)

    half = columns[0].shape[0] // 2
    part = ncol * half
    rows = 2 * part
    tiles = w_ref.shape[2] // LANES
    per = LANES // head_dim
    heads = tiles * per
    scale = 1.0 / math.sqrt(head_dim)

    def work():
        for f in range(2):
            for j in range(ncol):
                at = f * part + j * half
                x_ref[at : at + half, :] = columns[j][f * half : (f + 1) * half, :]
        lane = lax.broadcasted_iota(jnp.int32, (1, LANES), 1)
        for t in range(tiles):
            cols = slice(t * LANES, (t + 1) * LANES)
            if first:
                q = jnp.dot(x_ref[...], w_ref[0, :, cols], preferred_element_type=jnp.float32)
                q_new[:, cols] = (q.astype(jnp.bfloat16).astype(jnp.float32) * scale).astype(jnp.bfloat16)
                queries = q_new[:, cols]
            else:
                queries = q_old[:, cols]
            keys = jnp.dot(x_ref[...], w_ref[1, :, cols], preferred_element_type=jnp.float32).astype(jnp.bfloat16)
            values = jnp.dot(x_ref[...], w_ref[2, :, cols], preferred_element_type=jnp.float32).astype(jnp.bfloat16)
            for e in range(per):
                h = t * per + e
                inside = (lane >= e * head_dim) & (lane < (e + 1) * head_dim)
                ones_at = ((e + 1) % per) * head_dim
                filler = jnp.where(lane == ones_at, 1.0, 0.0).astype(jnp.bfloat16)
                head_q = jnp.where(inside, queries, jnp.zeros_like(queries))
                head_v = jnp.where(inside, values, jnp.broadcast_to(filler, values.shape))
                for f in range(2):
                    qs = slice(f * part, (f + 1) * part)
                    depth = (f + 1) * part if first else rows
                    scores = lax.dot_general(
                        head_q[qs], keys[:depth], (((1,), (1,)), ((), ())), preferred_element_type=jnp.float32
                    )
                    top = jnp.max(scores, axis=1, keepdims=True)
                    if not first:
                        before = top_old[qs, h : h + 1]
                        top = jnp.maximum(top, before)
                    weights = jnp.exp(scores - top).astype(jnp.bfloat16)
                    acc = jnp.dot(weights, head_v[:depth], preferred_element_type=jnp.float32)
                    if not first:
                        acc = acc + acc_old[h, qs, :] * jnp.exp(before - top)
                    acc_new[h, qs, :] = acc
                    top_new[qs, h : h + 1] = top

    if first:
        work()
    else:
        valid = valid_ref[0] > 0

        @pl.when(valid)
        def _():
            work()

        @pl.when(jnp.logical_not(valid))
        def _():
            acc_new[...] = acc_old[...]
            top_new[...] = top_old[...]

    if last:
        lane = lax.broadcasted_iota(jnp.int32, (1, LANES), 1)
        for t in range(tiles):
            result = None
            for e in range(per):
                h = t * per + e
                ones_at = ((e + 1) % per) * head_dim
                acc = acc_new[h]
                mine = acc / acc[:, ones_at : ones_at + 1]
                inside = (lane >= e * head_dim) & (lane < (e + 1) * head_dim)
                result = mine if result is None else jnp.where(inside, mine, result)
            result = result.astype(jnp.bfloat16)
            for f in range(2):
                for j in range(ncol):
                    at = f * part + j * half
                    outs[j][f * half : (f + 1) * half, t * LANES : (t + 1) * LANES] = result[at : at + half]


def attend_slab(columns, weights, state, valid, last, head_dim, name):
    ncol = len(columns)
    first = state is None
    crow, width = columns[0].shape
    rows = ncol * crow
    local = weights.shape[2]
    heads = local // head_dim
    q_shape = ((rows, local), jnp.bfloat16)
    acc_shape = ((heads, rows, LANES), jnp.float32)
    top_shape = ((rows, LANES), jnp.float32)
    outs, scratch = [], [pltpu.VMEM((rows, width), jnp.bfloat16)]
    if last:
        outs += [jax.ShapeDtypeStruct((crow, local), jnp.bfloat16)] * ncol
        scratch += [pltpu.VMEM(*acc_shape), pltpu.VMEM(*top_shape)]
        if first:
            scratch += [pltpu.VMEM(*q_shape)]
    else:
        if first:
            outs += [jax.ShapeDtypeStruct(*q_shape)]
        outs += [jax.ShapeDtypeStruct(*acc_shape), jax.ShapeDtypeStruct(*top_shape)]
    operands = ([] if first else [valid]) + list(columns) + [weights] + ([] if first else list(state))
    result = call(
        functools.partial(slab_kernel, ncol, first, last, head_dim),
        outs,
        operands,
        scratch=scratch,
        scalars=0 if first else 1,
        flops=2 * rows * width * 3 * local + 4 * heads * rows * rows * LANES,
        moved=weights.size * 2,
        name=name,
        limit=24,
    )
    if last:
        return result
    return result if first else [state[0]] + list(result)


def codes_kernel(pieces, at_ref, wanted_ref, *refs):
    blocks = refs[:pieces]
    ext_ref, chosen_ref, square_ref = refs[pieces:]
    depth, length = blocks[0].shape
    for i in range(pieces):
        start = pl.multiple_of(at_ref[i], length)
        block = blocks[i][...]
        block32 = block.astype(jnp.float32)
        squares = jnp.sum(block32 * block32, axis=0, keepdims=True)
        high = squares.astype(jnp.bfloat16)
        rest = squares - high.astype(jnp.float32)
        middle = rest.astype(jnp.bfloat16)
        low = (rest - middle.astype(jnp.float32)).astype(jnp.bfloat16)
        row = lax.broadcasted_iota(jnp.int32, (EXT - depth, length), 0)
        spread = lambda v: jnp.broadcast_to(v.astype(jnp.float32), row.shape)
        extra = jnp.where(row == 0, spread(high), jnp.where(row == 1, spread(middle), jnp.where(row == 2, spread(low), 0.0)))
        ext_ref[:depth, pl.ds(start, length)] = block
        ext_ref[depth:, pl.ds(start, length)] = extra.astype(jnp.bfloat16)
    tokens = wanted_ref.shape[0]
    lane = lax.broadcasted_iota(jnp.int32, (depth, LANES), 1)

    def pick(base):
        def one(i, so_far):
            code = wanted_ref[base + i]
            tile = ext_ref[:depth, pl.ds(pl.multiple_of(code // LANES * LANES, LANES), LANES)]
            turned = pltpu.roll(tile.astype(jnp.float32), lax.rem(i - lax.rem(code, LANES) + LANES, LANES), 1)
            return jnp.where(lane == i, turned, so_far)

        return lax.fori_loop(0, min(LANES, tokens - base), one, jnp.zeros((depth, LANES), jnp.float32), unroll=8)

    for base in range(0, tokens, LANES):
        chosen = pick(base)
        chosen_ref[:, base : base + LANES] = chosen
        square_ref[:, base : base + LANES] = jnp.sum(chosen * chosen, axis=0, keepdims=True)


def prepare_codes(pieces, starts, wanted, codes):
    depth = pieces[0].shape[0]
    tokens = -(-wanted.shape[0] // LANES) * LANES
    return call(
        functools.partial(codes_kernel, len(pieces)),
        [
            jax.ShapeDtypeStruct((EXT, codes), jnp.bfloat16),
            jax.ShapeDtypeStruct((depth, tokens), jnp.float32),
            jax.ShapeDtypeStruct((1, tokens), jnp.float32),
        ],
        [starts, wanted] + list(pieces),
        scalars=2,
        flops=codes * EXT * 200,
        moved=codes * EXT * 2,
        name="codes",
        limit=16,
    )


def tail_kernel(ncol, halves, order_ref, *refs):
    refs = list(refs)
    attended = [refs.pop(0) for _ in range(ncol)]
    matrices = [[refs.pop(0) for _ in range(halves[i])] for i in range(ncol)]
    block_ref, latent_w_ref, ext_ref, chosen_ref, square_ref = refs[:5]
    encoded_ref, least_ref, gap_ref = refs[5:8]
    joined = refs[8]
    rows, width = block_ref.shape
    total = jnp.zeros((rows, width), jnp.float32)
    for i in range(ncol):
        if halves[i] == 1:
            total += jnp.dot(attended[i][...], matrices[i][0][...], preferred_element_type=jnp.float32)
        else:
            size = matrices[i][0].shape[0]
            for k in range(halves[i]):
                joined[pl.ds(pl.multiple_of(order_ref[k] * size, size), size), :] = matrices[i][k][...]
            total += jnp.dot(attended[i][...], joined[...], preferred_element_type=jnp.float32)
    encoded = (block_ref[...].astype(jnp.float32) + total).astype(jnp.bfloat16)
    encoded_ref[...] = encoded
    depth = latent_w_ref.shape[0]
    latent_t = lax.dot_general(
        latent_w_ref[...], encoded, (((1,), (1,)), ((), ())), preferred_element_type=jnp.float32
    ).astype(jnp.bfloat16).astype(jnp.float32)
    own = jnp.sum(latent_t * latent_t, axis=0, keepdims=True)
    row = lax.broadcasted_iota(jnp.int32, (EXT - depth, rows), 0)
    full = jnp.concatenate([latent_t * -2.0, jnp.where(row < 3, 1.0, 0.0)], axis=0)
    left = full.T.astype(jnp.bfloat16)
    codes = ext_ref.shape[1]
    chunk = math.gcd(codes, 2048)

    def visit(i, least):
        dots = jnp.dot(left, ext_ref[:, pl.ds(pl.multiple_of(i * chunk, chunk), chunk)], preferred_element_type=jnp.float32)
        parts = [dots[:, c : c + LANES] for c in range(0, chunk, LANES)]
        while len(parts) > 1:
            parts = [jnp.minimum(a, b) for a, b in zip(parts[::2], parts[1::2])]
        return jnp.minimum(least, parts[0])

    least = lax.fori_loop(0, codes // chunk, visit, jnp.full((rows, LANES), 3e38, jnp.float32))
    least = jnp.min(least.T, axis=0, keepdims=True)
    nearest = (own + least) / depth
    cross = jnp.sum(latent_t * chosen_ref[:, :rows], axis=0, keepdims=True)
    reference = (own - 2.0 * cross + square_ref[:, :rows]) / depth
    least_ref[...] = nearest
    gap_ref[...] = reference - nearest


def shards(video, conv_weight, norm_gain, qkv_weight, out_weight, latent_weight, codebook, reference_codes):
    positions, frames_here, width = video.shape
    slabs, across, cores = (lax.axis_size(a) for a in ("frames", "code", "head"))
    sides = lax.axis_size("groups")
    slab, column, core, side = (lax.axis_index(a) for a in ("frames", "code", "head", "groups"))
    head_dim = width // HEADS
    rows = positions * frames_here

    own = jnp.transpose(video, (1, 0, 2)).reshape(rows, width)
    projection = jnp.transpose(qkv_weight, (1, 0, 2))
    gain = norm_gain.reshape(1, width)

    raw = [own]
    for d in range(1, slabs):
        raw.append(shifted(raw[-1], "frames", 1, False))
    raw.append(jnp.zeros_like(own))

    def shard_halves(array, axis):
        share = array.shape[axis] // sides
        mine = lax.dynamic_slice_in_dim(array, side * share, share, axis)
        pieces = []
        for dx in range(across):
            if dx == 0:
                got = [array]
            else:
                first = shifted(mine, "code", dx, True)
                got = [first] + [shifted(first, "groups", dy, True) for dy in range(1, sides)]
            pieces.append(got)
        result = []
        for dx in range(across):
            for dc in range(cores):
                result.append([g if dc == 0 else shifted(g, "head", dc, True) for g in pieces[dx]])
        return result

    matrices = shard_halves(out_weight, 0)
    code_pieces = shard_halves(codebook, 1)
    order = jnp.stack([lax.rem(side - dy + sides, sides) for dy in range(sides)]).astype(jnp.int32)
    shard_codes = codebook.shape[1]
    starts, flat = [], []
    for dx in range(across):
        for dc in range(cores):
            base = (lax.rem(column - dx + across, across) * cores + lax.rem(core - dc + cores, cores)) * shard_codes
            got = code_pieces[dx * cores + dc]
            if len(got) == 1:
                share = shard_codes // sides
                for y in range(sides):
                    flat.append(got[0][:, y * share : (y + 1) * share])
                    starts.append(base + y * share)
            else:
                for dy, piece in enumerate(got):
                    flat.append(piece)
                    starts.append(base + lax.rem(side - dy + sides, sides) * (shard_codes // sides))
    mine = lax.dynamic_slice_in_dim(reference_codes, (column * cores + core) * positions, positions, 0)
    wanted = jnp.transpose(mine).reshape(rows)
    extended, chosen, chosen_square = prepare_codes(
        flat, jnp.stack(starts).astype(jnp.int32), wanted, shard_codes * across * cores
    )

    def spread(columns):
        return [c if dc == 0 else shifted(c, "head", dc, True) for c in columns for dc in range(cores)]

    def exchanged(normed):
        return [shifted(normed, "code", dx, True) for dx in range(1, across)]

    state, outs, first_others = None, None, None
    for d in range(slabs):
        keep = d == 0
        result = conv_norm([(raw[d], raw[d + 1])], conv_weight, gain, keep, f"conv{d}")
        normed = result[0]
        if keep:
            block_input = result[1]
        if d == 0:
            others = first_others = exchanged(normed)
        elif d < slabs - 1:
            others = exchanged(normed)
        else:
            others = [lax.ppermute(o, "frames", [(0, slabs - 1)]) for o in first_others]
        valid = (slab >= d).astype(jnp.int32).reshape(1)
        state = attend_slab(
            spread([normed] + others), projection, state, valid, d == slabs - 1, head_dim, f"slab{d}"
        )
    outs = state

    returned = []
    for dx in range(across):
        for dc in range(cores):
            piece = outs[dx * cores + dc]
            if dc:
                piece = shifted(piece, "head", -dc, True)
            if dx:
                piece = shifted(piece, "code", -dx, True)
            returned.append(piece)
    def opposite(i):
        dx, dc = divmod(i, cores)
        return (-dx % across) * cores + (-dc % cores)

    meeting = [matrices[opposite(i)] for i in range(across * cores)]
    halves = [len(m) for m in meeting]
    encoded, least, gap = call(
        functools.partial(tail_kernel, across * cores, halves),
        [
            jax.ShapeDtypeStruct((rows, width), jnp.bfloat16),
            jax.ShapeDtypeStruct((1, rows), jnp.float32),
            jax.ShapeDtypeStruct((1, rows), jnp.float32),
        ],
        [order] + returned + [m for ms in meeting for m in ms]
        + [block_input, jnp.transpose(latent_weight), extended, chosen, chosen_square],
        scratch=[pltpu.VMEM(out_weight.shape, jnp.bfloat16)],
        scalars=1,
        flops=2 * rows * width * width + rows * extended.shape[1] * 128,
        moved=extended.size * 2 + width * width * 2,
        name="tail",
        limit=24,
    )
    split = lambda v: jnp.transpose(v.reshape(frames_here, positions))
    return (
        jnp.transpose(encoded.reshape(frames_here, positions, width), (1, 0, 2)),
        split(least),
        split(gap),
    )


def solution(mesh):
    return jax.shard_map(
        shards,
        mesh=mesh,
        in_specs=(
            P(("code", "head"), ("groups", "frames"), None),
            P(),
            P(),
            P(None, None, ("code", "head")),
            P(("code", "head"), None),
            P(),
            P(None, ("code", "head")),
            P(None, ("groups", "frames")),
        ),
        out_specs=(
            P(("code", "head"), ("groups", "frames"), None),
            P(("code", "head"), ("groups", "frames")),
            P(("code", "head"), ("groups", "frames")),
        ),
        check_vma=False,
    )
```
